32 devices in a mesh: seq: 8 (over z, x), pos: 4 (over y, core).
Axes of the slice: x: 2, y: 2, z: 4, core: 2. Of those that a mesh axis runs over, the one named last changes fastest.
Arguments:
- inputs: bfloat16 [8, 1024, 768], P('seq', 'pos'), may hold values from -6 to 6
- lengths: int32 [8], P('seq'), may hold values from 64 to 1024, as said below
- prenorm: bfloat16 [2, 768], P(None, ('seq', 'pos')), may hold values from 0.099609375 to 1.8984375
- value_proj: bfloat16 [2, 768, 768], P(None, ('seq', 'pos')), may hold values from -0.21875 to 0.21875
- mixing: bfloat16 [2, 12, 1024, 1024], P(None, 'pos', 'seq'), may hold values from -8 to 8
- out_proj: bfloat16 [2, 768, 768], P(None, ('seq', 'pos')), may hold values from -1.25 to 1.25
- ffn_gain: bfloat16 [2, 768], P(None, ('seq', 'pos')), may hold values from 0.099609375 to 1.8984375
- up_proj: bfloat16 [2, 768, 3072], P(None, ('seq', 'pos')), may hold values from -0.21875 to 0.21875
- down_proj: bfloat16 [2, 3072, 768], P(None, ('seq', 'pos')), may hold values from -0.109375 to 0.109375
- cotangent: bfloat16 [8, 1024, 768], P('seq', 'pos'), may hold values from -6 to 6
Outputs:
- outputs: bfloat16 [8, 1024, 768], P('seq', 'pos')
- input_grad: bfloat16 [8, 1024, 768], P('seq', 'pos')
- grad_prenorm: float32 [2, 768], P(None, ('seq', 'pos'))
- grad_value_proj: float32 [2, 768, 768], P(None, ('seq', 'pos'))
- grad_mixing: float32 [2, 12, 1024, 1024], P(None, 'pos', 'seq')
- grad_out_proj: float32 [2, 768, 768], P(None, ('seq', 'pos'))
- grad_ffn_gain: float32 [2, 768], P(None, ('seq', 'pos'))
- grad_up_proj: float32 [2, 768, 3072], P(None, ('seq', 'pos'))
- grad_down_proj: float32 [2, 3072, 768], P(None, ('seq', 'pos'))
The draws below stay inside these ranges and needn't reach their ends.
Inputs may be any that keep to these rules, and one draw needn't show every extreme that they name: `lengths`: some item has exactly 1024 valid positions and some exactly 64.
All inputs are finite; a program needn't handle non-finite values.
Results may differ from the reference program's by a relative error of at most 0.015.
Values may be sent and summed in bfloat16 or wider, within the bound.
A program may use at most 192 MiB of HBM per device.

```python
import math
import jax
import jax.numpy as jnp
from jax import lax

D = 768
HEADS = 12
HEAD_DIM = 64
FF = 3072
SLOT = 1024
MIN_LEN = 64
LAYERS = 2
SEQS = 8


def draw_lengths(key, part):
    first_key, second_key = jax.random.split(jax.random.fold_in(key, 17))
    values = jax.random.randint(first_key, (SEQS,), MIN_LEN, SLOT + 1, dtype=jnp.int32)
    order = jax.random.permutation(second_key, SEQS)
    values = values.at[order[0]].set(SLOT)
    values = values.at[order[1]].set(MIN_LEN)
    return values


def spiked(array, rng, source, target, blocks, factor):
    def block_of(dim):
        return (jnp.arange(array.shape[dim]) // (array.shape[dim] // blocks)).reshape((-1,) + (1,) * (array.ndim - 1 - dim))

    first = jax.random.permutation(rng, blocks)[block_of(target)]
    far = (block_of(target) + blocks // 2) % blocks
    return jnp.where((block_of(source) == first) | (block_of(source) == far), factor * array, array)


def block_scale(rng, shape, cuts, least, top_value):
    def one(dim, blocks):
        steps = jax.random.uniform(jax.random.fold_in(jax.random.fold_in(rng, 6), dim), (blocks,), jnp.float32, least / len(cuts), top_value / len(cuts))
        return jnp.repeat(jnp.exp(steps), shape[dim] // blocks).reshape((-1,) + (1,) * (len(shape) - dim - 1))

    level = one(*cuts[0])
    for cut in cuts[1:]:
        level = level * one(*cut)
    return level


def scatter_about(key, dims, deviation, limit, pieces=(), kind=jnp.bfloat16):
    drawn = jax.random.normal(key, dims, jnp.float32) * deviation
    if len(pieces) > 0:
        drawn = block_scale(key, dims, pieces, -0.22, 0.18) * drawn
    return jnp.clip(drawn, min=-limit, max=limit).astype(kind)


def heavy_noise(own_key, dims, spread, most, cuts, heavy, held_as=jnp.bfloat16):
    values = spread * jax.random.normal(own_key, dims, jnp.float32)
    if cuts:
        values = values * block_scale(own_key, dims, cuts, -0.22, 0.18)
    return jnp.clip(spiked(values, jax.random.fold_in(own_key, 3), *heavy), -most, most).astype(held_as)


def setup_inputs(seed: int = 0) -> dict:
    key_list = jax.random.split(jax.random.key(seed), 11)
    return {
        "inputs": heavy_noise(key_list[0], (SEQS, SLOT, D), 1.0, 6.0, ((0, 8), (1, 4)), (0, 2, 8, 2.0)),
        "lengths": draw_lengths(jax.random.fold_in(key_list[10], 71), 0),
        "prenorm": jnp.clip(1.0 + 0.18 * jax.random.normal(key_list[2], (LAYERS, D), jnp.float32), 0.099609375, 1.8984375).astype(jnp.bfloat16),
        "value_proj": scatter_about(key_list[3], (LAYERS, D, D), D ** -0.5, 0.21875, ((1, 32),)),
        "mixing": scatter_about(key_list[4], (LAYERS, HEADS, SLOT, SLOT), 1.5, 8.0, ((1, 4), (2, 8))),
        "out_proj": scatter_about(key_list[5], (LAYERS, D, D), (D // 32) ** -0.5, 1.25, ((1, 32),)),
        "ffn_gain": jnp.clip(1.0 + 0.18 * jax.random.normal(key_list[6], (LAYERS, D), jnp.float32), 0.099609375, 1.8984375).astype(jnp.bfloat16),
        "up_proj": scatter_about(key_list[7], (LAYERS, D, FF), D ** -0.5, 0.21875, ((1, 32),)),
        "down_proj": scatter_about(key_list[8], (LAYERS, FF, D), FF ** -0.5, 0.109375, ((1, 32),)),
        "cotangent": scatter_about(key_list[9], (SEQS, SLOT, D), 1.0, 6.0, ((0, 8), (1, 4))),
    }


epsilon = 1e-05

@jax.custom_vjp
def low(v):
    return lax.optimization_barrier(v.astype(jnp.bfloat16)).astype(jnp.float32)

@jax.custom_vjp
def low_back(v):
    return v

def low_keep(v):
    return (low(v), None)

def low_pass(kept, grad):
    return (grad,)

def back_keep(v):
    return (v, None)

def back_low(kept, grad):
    return (low(grad),)
low.defvjp(low_keep, low_pass)
low_back.defvjp(back_keep, back_low)

def rms_scale(values, gain):
    inverse = lax.rsqrt(lax.optimization_barrier(jnp.mean(values * values, axis=-1, keepdims=True)) + epsilon)
    return values * inverse * gain

def gelu_tanh(values):
    return jax.nn.gelu(values, approximate=True)

def mix_probs(logits, length):
    extent = logits.shape[-1]
    position = lax.iota(jnp.int32, extent)
    keep_column = position[None, None, :] < length
    keep_row = position[None, :, None] < length
    masked = jnp.where(keep_column, logits, -1e+30)
    highest = lax.optimization_barrier(jnp.max(masked, axis=-1, keepdims=True))
    raised = jnp.where(keep_column, jnp.exp(masked - highest), 0.0)
    shares = raised / lax.optimization_barrier(jnp.sum(raised, axis=-1, keepdims=True))
    return jnp.where(keep_row, shares, 0.0)

def project(left, right):
    return jnp.einsum('spd,de->spe', left, right, precision=lax.Precision.HIGHEST)

def one_layer(state, lengths, params, which):
    prenorm, value_proj, mixing, out_proj, ffn_gain, up_proj, down_proj = params
    seqs, slots, width = state.shape
    normed = low(rms_scale(state, prenorm[which]))
    valued = low_back(low(project(normed, value_proj[which])))
    by_heads = valued.reshape(seqs, slots, HEADS, HEAD_DIM)
    logits = mixing[which]
    mix_weights = low(jax.vmap(lambda length: mix_probs(logits, length))(lengths))
    mixed = jnp.einsum('shij,sjhd->sihd', mix_weights, by_heads, precision=lax.Precision.HIGHEST)
    mixed = low_back(low(mixed.reshape(seqs, slots, width)))
    middle = state + low_back(project(mixed, out_proj[which]))
    normed_ffn = low(rms_scale(middle, ffn_gain[which]))
    pre_act = low_back(project(normed_ffn, up_proj[which]))
    activated = low(gelu_tanh(pre_act))
    return middle + low_back(project(activated, down_proj[which]))

def block(params, inputs, lengths):
    position = lax.iota(jnp.int32, SLOT)
    live = (position[None, :] < lengths[:, None]).astype(jnp.float32)[:, :, None]
    state = inputs * live
    for which in range(LAYERS):
        state = one_layer(state, lengths, params, which)
    return state

def reference(inputs, lengths, prenorm, value_proj, mixing, out_proj, ffn_gain, up_proj, down_proj, cotangent):
    params = tuple((weight.astype(jnp.float32) for weight in (prenorm, value_proj, mixing, out_proj, ffn_gain, up_proj, down_proj)))
    group = math.gcd(SEQS, 4)
    shaped = inputs.astype(jnp.float32).reshape(SEQS // group, group, SLOT, D)
    grouped_lengths = lengths.reshape(SEQS // group, group)

    def run(weights, values):

        def per_group(pair):
            return block(weights, pair[0], pair[1])
        return lax.map(jax.checkpoint(per_group), (values, grouped_lengths))
    result, pullback = jax.vjp(run, params, shaped)
    grad_params, grad_inputs = pullback(cotangent.astype(jnp.float32).reshape(shaped.shape))
    return (result.reshape(SEQS, SLOT, D).astype(jnp.bfloat16), grad_inputs.reshape(SEQS, SLOT, D).astype(jnp.bfloat16), grad_params[0], grad_params[1], grad_params[2], grad_params[3], grad_params[4], grad_params[5], grad_params[6])
```

```python
import jax
import jax.numpy as jnp
from jax import lax
from jax.sharding import PartitionSpec as P

epsilon = 1e-05
both = ("seq", "pos")
bf16 = jnp.bfloat16
f32 = jnp.float32


def dot(spec, left, right):
    return jnp.einsum(spec, left, right, preferred_element_type=f32)


def rms_forward(values, gain):
    inverse = lax.rsqrt(jnp.mean(values * values, axis=-1, keepdims=True) + epsilon)
    return (values * inverse * gain).astype(bf16)


def rms_backward(values, gain, upstream):
    inverse = lax.rsqrt(jnp.mean(values * values, axis=-1, keepdims=True) + epsilon)
    scaled = values * inverse
    grad_gain = jnp.sum(upstream * scaled, axis=0)
    weighted = upstream * gain
    mean = jnp.mean(weighted * scaled, axis=-1, keepdims=True)
    return inverse * (weighted - scaled * mean), grad_gain


def gelu_parts(values):
    inner = 0.7978845608028654 * (values + 0.044715 * values * values * values)
    bent = jnp.tanh(inner)
    half = 0.5 * (1.0 + bent)
    slope = 0.7978845608028654 * (1.0 + 3.0 * 0.044715 * values * values)
    return values * half, half + 0.5 * values * (1.0 - bent * bent) * slope


def pack_weights(which, prenorm, value_proj, out_proj, ffn_gain, up_proj, down_proj):
    width = value_proj.shape[-1]
    pieces = up_proj.shape[-1] // width
    gains = jnp.concatenate([prenorm[which], ffn_gain[which]])
    gains = jnp.pad(gains[None, :], ((0, 7), (0, width - gains.shape[0])))
    ups = [up_proj[which][:, width * b : width * (b + 1)] for b in range(pieces)]
    return jnp.concatenate([value_proj[which], out_proj[which], *ups, down_proj[which], gains])


def unpack_weights(packed, rows, pieces):
    width = packed.shape[-1]
    value_w = packed[:, :rows].reshape(width, width)
    out_w = packed[:, rows : 2 * rows].reshape(width, width)
    ups = [
        packed[:, (2 + b) * rows : (3 + b) * rows].reshape(width, width) for b in range(pieces)
    ]
    low = (2 + pieces) * rows
    down_w = packed[:, low : low + pieces * rows].reshape(pieces * width, width)
    gains = packed[:, low + pieces * rows].astype(f32)
    gain = gains[:, :rows].reshape(width)
    gain_ffn = gains[:, rows : 2 * rows].reshape(width)
    return value_w, out_w, jnp.concatenate(ups, axis=1), down_w, gain, gain_ffn


def pack_grads(value_g, out_g, up_g, down_g, gain_g, gain_ffn_g, count):
    width = value_g.shape[-1]
    rows = width // count
    pieces = up_g.shape[-1] // width
    ups = [up_g[:, width * b : width * (b + 1)].reshape(count, rows, width) for b in range(pieces)]
    gains = jnp.concatenate(
        [gain_g.reshape(count, rows), gain_ffn_g.reshape(count, rows)], axis=1
    ).astype(bf16)
    gains = jnp.pad(gains[:, None, :], ((0, 0), (0, 7), (0, width - 2 * rows)))
    return jnp.concatenate(
        [
            value_g.reshape(count, rows, width),
            out_g.reshape(count, rows, width),
            *ups,
            down_g.reshape(count, pieces * rows, width),
            gains,
        ],
        axis=1,
    )


def unpack_grads(packed, rows, pieces):
    packed = packed.astype(f32)
    low = (2 + pieces) * rows
    ups = [packed[(2 + b) * rows : (3 + b) * rows] for b in range(pieces)]
    gains = packed[low + pieces * rows]
    return (
        gains[:rows],
        packed[:rows],
        packed[rows : 2 * rows],
        gains[rows : 2 * rows],
        jnp.concatenate(ups, axis=1),
        packed[low : low + pieces * rows],
    )


def local(
    inputs, lengths, prenorm, value_proj, mixing, out_proj, ffn_gain, up_proj, down_proj, cotangent
):
    layers, rows, width = value_proj.shape
    pieces = up_proj.shape[-1] // width
    count = width // rows
    slots_here = inputs.shape[1]
    heads = mixing.shape[1]
    slots = mixing.shape[3]
    head_dim = width // (heads * (slots // slots_here))
    position = lax.axis_index("pos") * slots_here + lax.iota(jnp.int32, slots_here)
    live = (position < lengths[0]).astype(f32)[:, None]
    all_lengths = lax.all_gather(lengths, "seq", axis=0, tiled=True)
    seqs = all_lengths.shape[0]
    mask = (lax.iota(jnp.int32, slots)[None, :] < all_lengths[:, None]).astype(f32)

    state = inputs[0].astype(f32) * live
    fetched = []
    stored = []
    for which in range(layers):
        packed = pack_weights(
            which, prenorm, value_proj, out_proj, ffn_gain, up_proj, down_proj
        )
        gathered = lax.all_gather(packed, both, axis=0)
        fetched.append(unpack_weights(gathered, rows, pieces))
    for which in range(layers):
        value_w, out_w, up_w, down_w, gain, gain_ffn = fetched[which]
        normed = rms_forward(state, gain)
        valued = dot("de,td->et", value_w, normed).astype(bf16)
        values = lax.all_to_all(valued, "pos", split_axis=0, concat_axis=1, tiled=True)
        values = lax.all_gather(values, "seq", axis=0)
        values = values.reshape(seqs, heads, head_dim, slots)
        raised = jnp.exp(mixing[which].astype(f32)).astype(bf16)
        totals = dot("sj,hij->shi", mask.astype(bf16), raised)
        inverse = 1.0 / totals
        mixed = dot("shdj,hij->shdi", values, raised) * inverse[:, :, None, :]
        mixed = mixed.astype(bf16)
        back = mixed.reshape(seqs, heads * head_dim, mixed.shape[-1])
        back = lax.all_to_all(back, "seq", split_axis=0, concat_axis=2, tiled=True)[0]
        back = lax.all_to_all(back, "pos", split_axis=1, concat_axis=0, tiled=True)
        returned = (back.T.astype(f32) * live).astype(bf16)
        middle = state + dot("td,de->te", returned, out_w)
        normed_ffn = rms_forward(middle, gain_ffn)
        pre_act = dot("td,df->tf", normed_ffn, up_w)
        activated = gelu_parts(pre_act)[0].astype(bf16)
        stored.append(
            (state, normed, values, raised, inverse, mixed, returned, middle, normed_ffn, pre_act)
        )
        state = middle + dot("tf,fd->td", activated, down_w)

    upstream = cotangent[0].astype(f32) * live
    outcomes = [None] * layers
    logit_grads = [None] * layers
    for which in reversed(range(layers)):
        value_w, out_w, up_w, down_w, gain, gain_ffn = fetched[which]
        before, normed, values, raised, inverse, mixed, returned, middle, normed_ffn, pre_act = (
            stored[which]
        )
        grad_ffn = upstream.astype(bf16)
        activated, slope = gelu_parts(pre_act)
        grad_down = dot("tf,td->fd", activated.astype(bf16), grad_ffn).astype(bf16)
        grad_pre = (dot("td,fd->tf", grad_ffn, down_w) * slope).astype(bf16)
        grad_up = dot("td,tf->df", normed_ffn, grad_pre).astype(bf16)
        step, grad_gain_ffn = rms_backward(middle, gain_ffn, dot("tf,df->td", grad_pre, up_w))
        grad_middle = upstream + step
        grad_mid = grad_middle.astype(bf16)
        grad_out = dot("td,te->de", returned, grad_mid).astype(bf16)
        grad_mixed = dot("ed,td->et", out_w, grad_mid).astype(bf16)
        sent = lax.all_to_all(grad_mixed, "pos", split_axis=0, concat_axis=1, tiled=True)
        sent = sent[None]
        grads = lax.all_to_all(sent, "seq", split_axis=2, concat_axis=0, tiled=True)
        grads = grads.reshape(mixed.shape).astype(f32)
        row_sums = jnp.sum(grads * mixed.astype(f32), axis=2) * inverse
        scaled = (grads * inverse[:, :, None, :]).astype(bf16)
        table = dot("shdi,shdj->hij", scaled, values)
        table = table - jnp.einsum(
            "shi,sj->hij", row_sums, mask, precision=lax.Precision.HIGHEST
        )
        logit_grads[which] = raised.astype(f32) * table
        partial = (dot("shdi,hij->shdj", scaled, raised) * mask[:, None, None, :]).astype(bf16)
        partial = partial.reshape(seqs, heads * head_dim, slots)
        summed = lax.psum_scatter(partial, "seq", scatter_dimension=0, tiled=True)[0]
        grad_valued = lax.all_to_all(summed, "pos", split_axis=1, concat_axis=0, tiled=True)
        grad_value = dot("td,et->de", normed, grad_valued).astype(bf16)
        step, grad_gain = rms_backward(before, gain, dot("et,de->td", grad_valued, value_w))
        upstream = grad_middle + step
        packed = pack_grads(
            grad_value, grad_out, grad_up, grad_down, grad_gain, grad_gain_ffn, count
        )
        reduced = lax.psum_scatter(packed, both, scatter_dimension=0, tiled=True)[0]
        outcomes[which] = unpack_grads(reduced, rows, pieces)
    merged = [jnp.stack([terms[member] for terms in outcomes]) for member in range(6)]
    return (
        state.astype(bf16)[None],
        (upstream * live).astype(bf16)[None],
        merged[0],
        merged[1],
        jnp.stack(logit_grads),
        merged[2],
        merged[3],
        merged[4],
        merged[5],
    )


def solution(mesh):
    return jax.shard_map(
        local,
        mesh=mesh,
        in_specs=(
            P("seq", "pos", None),
            P("seq"),
            P(None, ("seq", "pos")),
            P(None, ("seq", "pos"), None),
            P(None, "pos", "seq", None),
            P(None, ("seq", "pos"), None),
            P(None, ("seq", "pos")),
            P(None, ("seq", "pos"), None),
            P(None, ("seq", "pos"), None),
            P("seq", "pos", None),
        ),
        out_specs=(
            P("seq", "pos", None),
            P("seq", "pos", None),
            P(None, ("seq", "pos")),
            P(None, ("seq", "pos"), None),
            P(None, "pos", "seq", None),
            P(None, ("seq", "pos"), None),
            P(None, ("seq", "pos")),
            P(None, ("seq", "pos"), None),
            P(None, ("seq", "pos"), None),
        ),
        check_vma=False,
    )
```

```python
import functools
import jax
import jax.numpy as jnp
from jax import lax
from jax.experimental import pallas as pl
from jax.experimental.pallas import tpu as pltpu
from jax.sharding import PartitionSpec as P

epsilon = 1e-05
both = ("seq", "pos")
bf16 = jnp.bfloat16
f32 = jnp.float32
MESH = pl.DeviceIdType.MESH


def own_place():
    seq = lax.axis_index("seq")
    pos = lax.axis_index("pos")
    z = lax.div(seq, 2)
    y = lax.div(pos, 2)
    return z, seq - 2 * z, y, pos - 2 * y


def device_of(place):
    z, x, y, c = place
    return (2 * z + x, 2 * y + c)


def order_of(place):
    z, x, y, c = place
    return 4 * (2 * z + x) + 2 * y + c


def across(place, axis):
    z, x, y, c = place
    if axis == "x":
        return z, 1 - x, y, c
    if axis == "y":
        return z, x, 1 - y, c
    if axis == "xy":
        return z, 1 - x, 1 - y, c
    if axis == "core":
        return z, x, y, 1 - c
    if axis == "first":
        return z, x + (1 - c) * (1 - 2 * x), y + c * (1 - 2 * y), c
    if axis == "second":
        return z, x + c * (1 - 2 * x), y + (1 - c) * (1 - 2 * y), c
    if axis == "up":
        return z + 1, x, y, c
    return z - 1, x, y, c


def shifted(place, step):
    z, x, y, c = place
    return z + step, x, y, c


def greet(place, axes):
    barrier = pltpu.get_barrier_semaphore()
    z = place[0]

    def tell(axis):
        pl.semaphore_signal(
            barrier, inc=1, device_id=device_of(across(place, axis)), device_id_type=MESH
        )

    for axis in axes:
        tell(axis)
    pl.when(z < 3)(lambda: tell("up"))
    pl.when(z > 0)(lambda: tell("down"))
    ends = jnp.where(z == 0, 1, 0) + jnp.where(z == 3, 1, 0)
    pl.semaphore_wait(barrier, len(axes) + 2 - ends)


class Flow:
    def __init__(self, place, send, recv):
        self.place = place
        self.send = send
        self.recv = recv
        self.sent = []

    def push(self, kind, axis, source, target, name, when=None):
        there = device_of(across(self.place, axis))

        def go(act):
            copy = pltpu.make_async_remote_copy(
                src_ref=source,
                dst_ref=target,
                send_sem=self.send.at[kind, name],
                recv_sem=self.recv.at[name],
                device_id=there,
                device_id_type=MESH,
            )
            act(copy)

        def guarded(act):
            if when is None:
                go(act)
            else:
                pl.when(when)(lambda: go(act))

        guarded(lambda copy: copy.start())
        self.sent.append(guarded)

    def arrived(self, target, name):
        pltpu.make_async_remote_copy(
            src_ref=target,
            dst_ref=target,
            send_sem=self.send.at[0, name],
            recv_sem=self.recv.at[name],
            device_id=device_of(across(self.place, "core")),
            device_id_type=MESH,
        ).wait_recv()

    def finish(self):
        for guarded in self.sent:
            guarded(lambda copy: copy.wait_send())


UP, DOWN, FIRST, SECOND, CORE = range(5)


class WeightGather(Flow):
    def __init__(self, place, own, out, send, recv):
        super().__init__(place, send, recv)
        self.own = own
        self.out = out

    def spread(self, origin, source, line=None, second=True, first=True, when=None):
        name = order_of(origin)
        target = self.out.at[name]
        z = self.place[0]
        for kind, axis, guard in ((UP, "up", z < 3), (DOWN, "down", z > 0)):
            if line is not None and axis in line:
                both = guard if when is None else guard & when
                self.push(kind, axis, source, target, name, both)
        if second:
            self.push(SECOND, "second", source, target, name, when)
        if first:
            self.push(FIRST, "first", source, target, name, when)
        self.push(CORE, "core", source, target, name, when)

    def begin(self):
        self.spread(self.place, self.own, line=("up", "down"))

    def line_step(self, step):
        z = self.place[0]
        for sign, line in ((-1, "up"), (1, "down")):
            origin = shifted(self.place, sign * step)
            valid = (origin[0] >= 0) & (origin[0] <= 3)
            name = order_of(origin)
            pl.when(valid)(lambda n=name: self.arrived(self.out.at[n], n))
            self.spread(origin, self.out.at[name], line=(line,), when=valid)

    def each(self, base, step):
        if step == 0:
            yield base, None
            return
        for sign in (-1, 1):
            origin = shifted(base, sign * step)
            yield origin, (origin[0] >= 0) & (origin[0] <= 3)

    def take(self, axis, step, first):
        base = across(self.place, axis)
        for origin, valid in self.each(base, step):
            name = order_of(origin)
            target = self.out.at[name]
            if valid is None:
                self.arrived(target, name)
            else:
                pl.when(valid)(lambda t=target, n=name: self.arrived(t, n))
            if first:
                self.push(FIRST, "first", target, target, name, valid)
            self.push(CORE, "core", target, target, name, valid)

    def second_step(self, step):
        self.take("second", step, True)

    def first_step(self, step):
        self.take("first", step, False)
        base = across(across(self.place, "first"), "second")
        for origin, valid in self.each(base, step):
            name = order_of(origin)
            target = self.out.at[name]
            if valid is None:
                self.arrived(target, name)
            else:
                pl.when(valid)(lambda t=target, n=name: self.arrived(t, n))
            self.push(CORE, "core", target, target, name, valid)

    def end(self):
        z, x, y, c = self.place
        for q in range(8):
            for yy in range(2):
                name = 4 * q + 2 * yy + 1 - c
                self.arrived(self.out.at[name], name)


class ValueGather(Flow):
    def __init__(self, place, blocks, out, send, recv):
        super().__init__(place, send, recv)
        self.blocks = blocks
        self.out = out

    def spot(self, origin):
        z, x, y, c = origin
        rows = self.blocks.shape[2]
        columns = self.blocks.shape[3]
        return self.out.at[
            :,
            pl.ds(pl.multiple_of((2 * z + x) * rows, rows), rows),
            pl.ds(pl.multiple_of((2 * y + c) * columns, columns), columns),
        ]

    def begin(self):
        z, x, y, c = self.place
        spot = self.spot(self.place)
        name = order_of(self.place)
        for kind, axis in enumerate(("xy", "x", "y")):
            there = across(self.place, axis)
            self.push(UP + kind, axis, self.blocks.at[2 * there[2] + there[1]], spot, name)
        mine = self.blocks.at[2 * y + x]
        self.relay(self.place, mine, ("up", "down"), kinds=(3, 4, 5))

    def keep(self, sem):
        z, x, y, c = self.place
        return pltpu.make_async_copy(self.blocks.at[2 * y + x], self.spot(self.place), sem)

    def relay(self, origin, source, line, when=None, kinds=(UP, DOWN, 2)):
        z = self.place[0]
        name = order_of(origin)
        target = self.spot(origin)
        for kind, axis, guard in ((kinds[0], "up", z < 3), (kinds[1], "down", z > 0)):
            if axis in line:
                both = guard if when is None else guard & when
                self.push(kind, axis, source, target, name, both)
        self.push(kinds[2], "core", source, target, name, when)

    def plane(self):
        for axis in ("x", "y", "xy"):
            origin = across(self.place, axis)
            spot = self.spot(origin)
            self.arrived(spot, order_of(origin))
            self.relay(origin, spot, ("up", "down"))

    def line_step(self, step):
        for sign, line in ((-1, "up"), (1, "down")):
            base = shifted(self.place, sign * step)
            valid = (base[0] >= 0) & (base[0] <= 3)
            for axis in ("", "x", "y", "xy"):
                origin = base if axis == "" else across(base, axis)
                spot = self.spot(origin)
                name = order_of(origin)
                pl.when(valid)(lambda s=spot, n=name: self.arrived(s, n))
                self.relay(origin, spot, (line,), when=valid)

    def end(self):
        z, x, y, c = self.place
        for q in range(8):
            for yy in range(2):
                origin = (q // 2, q % 2, yy, 1 - c)
                self.arrived(self.spot(origin), order_of(origin))


def gather_kernel(with_values, own, *refs):
    place = own_place()
    if with_values:
        blocks, out, values, send_w, recv_w, send_v, recv_v, local = refs
        value_flow = ValueGather(place, blocks, values, send_v, recv_v)
        kept = value_flow.keep(local.at[1])
    else:
        out, send_w, recv_w, local = refs
    weight_flow = WeightGather(place, own, out, send_w, recv_w)
    stay = pltpu.make_async_copy(own, out.at[order_of(place)], local.at[0])
    stay.start()
    if with_values:
        kept.start()
    greet(place, ("x", "y", "core") + (("xy",) if with_values else ()))
    weight_flow.begin()
    if with_values:
        value_flow.begin()
        value_flow.plane()
    weight_flow.line_step(1)
    if with_values:
        value_flow.line_step(1)
    weight_flow.second_step(0)
    weight_flow.line_step(2)
    if with_values:
        value_flow.line_step(2)
    weight_flow.second_step(1)
    weight_flow.first_step(0)
    weight_flow.line_step(3)
    weight_flow.second_step(2)
    weight_flow.first_step(1)
    if with_values:
        value_flow.line_step(3)
    weight_flow.second_step(3)
    weight_flow.first_step(2)
    weight_flow.first_step(3)
    if with_values:
        value_flow.end()
    weight_flow.end()
    stay.wait()
    if with_values:
        kept.wait()
        value_flow.finish()
    weight_flow.finish()


def gather(packed, blocks, collective_id):
    anywhere = pl.BlockSpec(memory_space=pl.ANY)
    with_values = blocks is not None
    out_shape = [jax.ShapeDtypeStruct((32,) + packed.shape, packed.dtype)]
    scratch = [pltpu.SemaphoreType.DMA((5, 32)), pltpu.SemaphoreType.DMA((32,))]
    operands = [packed]
    if with_values:
        groups, heads, size, columns = blocks.shape
        out_shape.append(jax.ShapeDtypeStruct((heads, 8 * size, 4 * columns), blocks.dtype))
        scratch += [pltpu.SemaphoreType.DMA((6, 32)), pltpu.SemaphoreType.DMA((32,))]
        operands.append(blocks)
    scratch.append(pltpu.SemaphoreType.DMA((2,)))
    return pl.pallas_call(
        functools.partial(gather_kernel, with_values),
        out_shape=out_shape,
        in_specs=[anywhere] * len(operands),
        out_specs=[anywhere] * len(out_shape),
        scratch_shapes=scratch,
        compiler_params=pltpu.CompilerParams(collective_id=collective_id, has_side_effects=True),
    )(*operands)


def line_order(z):
    high = lax.div(z, 2)
    return (3 - 3 * high, 2 - high, 1 - z + 4 * high, z)


def slot_of(place):
    z, x, y, c = place
    return 4 * z + 2 * x + y


class Reduce(Flow):
    def load(self, source, slot):
        return pltpu.make_async_copy(source, self.mine.at[slot], self.loaded.at[slot])

    def wait_slot(self, buffer, kind, slot):
        pltpu.make_async_remote_copy(
            src_ref=buffer.at[slot],
            dst_ref=buffer.at[slot],
            send_sem=self.send.at[kind, slot],
            recv_sem=self.recv.at[kind, slot],
            device_id=device_of(across(self.place, "core")),
            device_id_type=MESH,
        ).wait_recv()

    def push_slot(self, kind, axis, source, target, slot, when=None):
        there = device_of(across(self.place, axis))

        def guarded(act):
            def go():
                act(
                    pltpu.make_async_remote_copy(
                        src_ref=source,
                        dst_ref=target,
                        send_sem=self.send.at[kind, slot],
                        recv_sem=self.recv.at[kind, slot],
                        device_id=there,
                        device_id_type=MESH,
                    )
                )

            if when is None:
                go()
            else:
                pl.when(when)(go)

        guarded(lambda copy: copy.start())
        self.sent.append(guarded)

    def total(self, slot, buffers, out=None):
        rows = self.mine.shape[1]
        step = self.step

        def body(j, carry):
            part = pl.ds(pl.multiple_of(j * step, step), step)
            value = self.mine[slot, part].astype(f32)
            for buffer in buffers:
                value = value + buffer[slot, part].astype(f32)
            if out is None:
                self.mine[slot, part] = value.astype(self.mine.dtype)
            else:
                out[part] = value.astype(out.dtype)
            return carry

        lax.fori_loop(0, rows // step, body, 0)

    def line(self, there, slot, buffers, last):
        z = self.place[0]
        below, above = self.below, self.above

        @pl.when((there > z) & (z > 0))
        def _():
            self.wait_slot(below, 3, slot)
            self.total(slot, buffers + [below])

        @pl.when((there > z) & (z == 0))
        def _():
            self.total(slot, buffers)

        @pl.when((there < z) & (z < 3))
        def _():
            self.wait_slot(above, 4, slot)
            self.total(slot, buffers + [above])

        @pl.when((there < z) & (z == 3))
        def _():
            self.total(slot, buffers)

        self.push_slot(3, "up", self.mine.at[slot], below.at[slot], slot, there > z)
        self.push_slot(4, "down", self.mine.at[slot], above.at[slot], slot, there < z)

    def close(self, slot, buffers, out=None):
        z = self.place[0]

        @pl.when(z > 0)
        def _():
            self.wait_slot(self.below, 3, slot)

        @pl.when(z < 3)
        def _():
            self.wait_slot(self.above, 4, slot)

        @pl.when(z == 0)
        def _():
            self.total(slot, buffers + [self.above], out)

        @pl.when(z == 3)
        def _():
            self.total(slot, buffers + [self.below], out)

        @pl.when((z > 0) & (z < 3))
        def _():
            self.total(slot, buffers + [self.below, self.above], out)


class WeightReduce(Reduce):
    def __init__(self, place, packed, out, mine, partner, first, second, below, above, send, recv, loaded):
        super().__init__(place, send, recv)
        self.packed, self.out, self.mine, self.partner = packed, out, mine, partner
        self.first, self.second, self.below, self.above = first, second, below, above
        self.loaded = loaded
        rows = mine.shape[1]
        self.step = next(s for s in (48, 80, 112, 32, 16) if rows % s == 0)

    def group(self, place, which):
        base = place
        if which in "AB":
            base = across(base, "first")
        if which in "AC":
            base = across(base, "second")
        return [(there,) + base[1:] for there in line_order(place[0])]

    def begin(self, which):
        partner = across(self.place, "core")
        for goal in self.group(partner, which):
            slot = slot_of(goal)
            self.push_slot(
                0, "core", self.packed.at[order_of(goal)], self.partner.at[slot], slot
            )
        for goal in self.group(self.place, which):
            self.load(self.packed.at[order_of(goal)], slot_of(goal)).start()

    def ready(self, goal, kinds):
        slot = slot_of(goal)
        self.load(self.packed.at[order_of(goal)], slot).wait()
        buffers = [self.partner, self.first, self.second][:kinds]
        for kind, buffer in enumerate(buffers):
            self.wait_slot(buffer, kind, slot)
        return slot, buffers

    def far(self, which):
        for goal in self.group(self.place, which):
            slot, buffers = self.ready(goal, 1)
            self.total(slot, buffers)
            self.push_slot(1, "first", self.mine.at[slot], self.first.at[slot], slot)

    def near(self):
        for goal in self.group(self.place, "C"):
            slot, buffers = self.ready(goal, 2)
            self.total(slot, buffers)
            self.push_slot(2, "second", self.mine.at[slot], self.second.at[slot], slot)

    def column(self):
        goals = self.group(self.place, "D")
        for goal in goals[:3]:
            slot, buffers = self.ready(goal, 3)
            self.line(goal[0], slot, buffers, None)
        slot, buffers = self.ready(goals[3], 3)
        self.close(slot, buffers, self.out)


class ValueReduce(Reduce):
    def __init__(self, place, partial, out, mine, partner, below, above, send, recv, loaded, landed, kept):
        super().__init__(place, send, recv)
        self.partial, self.out, self.mine, self.partner = partial, out, mine, partner
        self.below, self.above, self.loaded, self.landed, self.kept = below, above, loaded, landed, kept
        self.step = mine.shape[1]

    def spot(self, goal):
        z, x, y, c = goal
        rows = self.mine.shape[2]
        columns = self.mine.shape[3]
        return self.partial.at[
            :,
            pl.ds(pl.multiple_of((2 * z + x) * rows, rows), rows),
            pl.ds(pl.multiple_of((2 * y + c) * columns, columns), columns),
        ]

    def group(self, place, k):
        z, x, y, c = place
        there = line_order(z)[k]
        return [(there, xx, yy, c) for xx in range(2) for yy in range(2)]

    def begin(self, k):
        for goal in self.group(across(self.place, "core"), k):
            slot = slot_of(goal)
            self.push_slot(0, "core", self.spot(goal), self.partner.at[slot], slot)
        for goal in self.group(self.place, k):
            self.load(self.spot(goal), slot_of(goal)).start()

    def ready(self, goal):
        slot = slot_of(goal)
        self.load(self.spot(goal), slot).wait()
        self.wait_slot(self.partner, 0, slot)
        return slot

    def pass_on(self, k):
        for goal in self.group(self.place, k):
            slot = self.ready(goal)
            self.line(goal[0], slot, [self.partner], None)

    def land(self):
        z, x, y, c = self.place
        own = 2 * y + x
        for axis in ("xy", "x", "y", ""):
            goal = self.place if axis == "" else across(self.place, axis)
            slot = self.ready(goal)
            self.close(slot, [self.partner])
            if axis == "":
                self.stay = pltpu.make_async_copy(
                    self.mine.at[slot], self.out.at[own], self.kept.at[0]
                )
                self.stay.start()
            else:
                kind = {"xy": 0, "x": 1, "y": 2}[axis]
                copy = pltpu.make_async_remote_copy(
                    src_ref=self.mine.at[slot],
                    dst_ref=self.out.at[own],
                    send_sem=self.kept.at[1 + kind],
                    recv_sem=self.landed.at[kind],
                    device_id=device_of(goal),
                    device_id_type=MESH,
                )
                copy.start()
                self.sent.append(lambda act, copy=copy: act(copy))

    def end(self):
        for kind, axis in enumerate(("xy", "x", "y")):
            z, x, y, c = across(self.place, axis)
            target = self.out.at[2 * y + x]
            pltpu.make_async_remote_copy(
                src_ref=target,
                dst_ref=target,
                send_sem=self.kept.at[1 + kind],
                recv_sem=self.landed.at[kind],
                device_id=device_of((z, x, y, c)),
                device_id_type=MESH,
            ).wait_recv()
        self.stay.wait()


def reduce_kernel(with_values, packed, *refs):
    place = own_place()
    if with_values:
        partial, out, values, *rest = refs
        wide, rest = rest[:9], rest[9:]
        value_flow = ValueReduce(place, partial, values, *rest)
    else:
        out, *wide = refs
    weight_flow = WeightReduce(place, packed, out, *wide)
    greet(place, ("x", "y", "core") + (("xy",) if with_values else ()))
    for k, which in enumerate("ABCD"):
        if with_values:
            value_flow.begin(k)
        weight_flow.begin(which)
    weight_flow.far("A")
    if with_values:
        value_flow.pass_on(0)
    weight_flow.far("B")
    if with_values:
        value_flow.pass_on(1)
    weight_flow.near()
    if with_values:
        value_flow.pass_on(2)
    weight_flow.column()
    if with_values:
        value_flow.land()
        value_flow.end()
        value_flow.finish()
    weight_flow.finish()


def reduce(packed, partial, collective_id):
    anywhere = pl.BlockSpec(memory_space=pl.ANY)
    with_values = partial is not None
    _, rows, width = packed.shape
    out_shape = [jax.ShapeDtypeStruct((rows, width), f32)]
    out_specs = [pl.BlockSpec(memory_space=pltpu.VMEM)]
    dma = pltpu.SemaphoreType.DMA
    scratch = [pltpu.VMEM((16, rows, width), bf16) for _ in range(6)]
    scratch += [dma((5, 16)), dma((5, 16)), dma((16,))]
    operands = [packed]
    if with_values:
        heads, tall, long = partial.shape
        block = (heads, tall // 8, long // 4)
        out_shape.append(jax.ShapeDtypeStruct((4,) + block, bf16))
        out_specs.append(anywhere)
        scratch += [pltpu.VMEM((16,) + block, bf16) for _ in range(4)]
        scratch += [dma((5, 16)), dma((5, 16)), dma((16,)), dma((3,)), dma((4,))]
        operands.append(partial)
    return pl.pallas_call(
        functools.partial(reduce_kernel, with_values),
        out_shape=out_shape,
        in_specs=[anywhere] * len(operands),
        out_specs=out_specs,
        scratch_shapes=scratch,
        compiler_params=pltpu.CompilerParams(
            collective_id=collective_id, has_side_effects=True, vmem_limit_bytes=60000 * 1024
        ),
    )(*operands)


def trade_kernel(to_rows, source, out, send, recv, local):
    place = own_place()
    z, x, y, c = place
    seq, pos = 2 * z + x, 2 * y + c
    width = out.shape[3] if to_rows else source.shape[3]

    def wide(ref, group, half):
        return ref.at[group, :, :, pl.ds(pl.multiple_of(half * width, width), width)]

    by_items = [((q // 2, q % 2, lax.div(z, 2), z - 2 * lax.div(z, 2)), q) for q in range(8)]
    by_parts = [((pos, g % 2, g // 2, half), 2 * g + half) for g in range(4) for half in range(2)]
    goals, origins = (by_parts, by_items) if to_rows else (by_items, by_parts)
    own_name = seq if to_rows else 2 * (2 * y + x) + c

    def is_own(there):
        return order_of(there) == order_of(place)

    barrier = pltpu.get_barrier_semaphore()
    for there, _ in origins:

        @pl.when(jnp.logical_not(is_own(there)))
        def _(there=there):
            pl.semaphore_signal(barrier, inc=1, device_id=device_of(there), device_id_type=MESH)

    pl.semaphore_wait(barrier, 8 - jnp.where(pos == z, 1, 0))

    def ends(name):
        if to_rows:
            return wide(source, name // 2, name % 2), out.at[:, seq]
        return source.at[:, name], wide(out, 2 * y + x, c)

    def landing(name):
        if to_rows:
            return out.at[:, name]
        return wide(out, name // 2, name % 2)

    def remote(there, name):
        begin, end = ends(name)
        return pltpu.make_async_remote_copy(
            src_ref=begin,
            dst_ref=end,
            send_sem=send.at[name],
            recv_sem=recv.at[own_name],
            device_id=device_of(there),
            device_id_type=MESH,
        )

    def here(name):
        begin, end = ends(name)
        return pltpu.make_async_copy(begin, end, local)

    for there, name in goals:
        own = is_own(there)
        pl.when(jnp.logical_not(own))(lambda: remote(there, name).start())
        pl.when(own)(lambda: here(name).start())
    for there, name in origins:
        target = landing(name)

        @pl.when(jnp.logical_not(is_own(there)))
        def _(target=target, name=name, there=there):
            pltpu.make_async_remote_copy(
                src_ref=target,
                dst_ref=target,
                send_sem=send.at[name],
                recv_sem=recv.at[name],
                device_id=device_of(there),
                device_id_type=MESH,
            ).wait_recv()

    for there, name in goals:
        own = is_own(there)
        pl.when(jnp.logical_not(own))(lambda: remote(there, name).wait_send())
        pl.when(own)(lambda: here(name).wait())


def trade(array, to_rows, collective_id):
    anywhere = pl.BlockSpec(memory_space=pl.ANY)
    if to_rows:
        _, heads, size, positions = array.shape
        shape = (heads, 8, size, positions // 2)
    else:
        heads, _, size, positions = array.shape
        shape = (4, heads, size, positions * 2)
    dma = pltpu.SemaphoreType.DMA
    return pl.pallas_call(
        functools.partial(trade_kernel, to_rows),
        out_shape=jax.ShapeDtypeStruct(shape, array.dtype),
        in_specs=[anywhere],
        out_specs=anywhere,
        scratch_shapes=[dma((8,)), dma((8,)), dma],
        compiler_params=pltpu.CompilerParams(collective_id=collective_id, has_side_effects=True),
    )(array)


def dot(spec, left, right):
    return jnp.einsum(spec, left, right, preferred_element_type=f32)


def rms_forward(values, gain):
    inverse = lax.rsqrt(jnp.mean(values * values, axis=-1, keepdims=True) + epsilon)
    return (values * inverse * gain).astype(bf16)


def rms_backward(values, gain, upstream):
    inverse = lax.rsqrt(jnp.mean(values * values, axis=-1, keepdims=True) + epsilon)
    scaled = values * inverse
    grad_gain = jnp.sum(upstream * scaled, axis=0)
    weighted = upstream * gain
    mean = jnp.mean(weighted * scaled, axis=-1, keepdims=True)
    return inverse * (weighted - scaled * mean), grad_gain


def gelu_parts(values):
    inner = 0.7978845608028654 * (values + 0.044715 * values * values * values)
    bent = jnp.tanh(inner)
    half = 0.5 * (1.0 + bent)
    slope = 0.7978845608028654 * (1.0 + 3.0 * 0.044715 * values * values)
    return values * half, half + 0.5 * values * (1.0 - bent * bent) * slope


def pack_weights(which, prenorm, value_proj, out_proj, ffn_gain, up_proj, down_proj):
    width = value_proj.shape[-1]
    pieces = up_proj.shape[-1] // width
    gains = jnp.concatenate([prenorm[which], ffn_gain[which]])
    gains = jnp.pad(gains[None, :], ((0, 7), (0, width - gains.shape[0])))
    ups = [up_proj[which][:, width * b : width * (b + 1)] for b in range(pieces)]
    return jnp.concatenate([value_proj[which], out_proj[which], *ups, down_proj[which], gains])


def unpack_weights(packed, rows, pieces):
    width = packed.shape[-1]
    value_w = packed[:, :rows].reshape(width, width)
    out_w = packed[:, rows : 2 * rows].reshape(width, width)
    ups = [
        packed[:, (2 + b) * rows : (3 + b) * rows].reshape(width, width) for b in range(pieces)
    ]
    low = (2 + pieces) * rows
    down_w = packed[:, low : low + pieces * rows].reshape(pieces * width, width)
    gains = packed[:, low + pieces * rows].astype(f32)
    gain = gains[:, :rows].reshape(width)
    gain_ffn = gains[:, rows : 2 * rows].reshape(width)
    return value_w, out_w, jnp.concatenate(ups, axis=1), down_w, gain, gain_ffn


def pack_grads(value_g, out_g, up_g, down_g, gain_g, gain_ffn_g, count):
    width = value_g.shape[-1]
    rows = width // count
    pieces = up_g.shape[-1] // width
    ups = [up_g[:, width * b : width * (b + 1)].reshape(count, rows, width) for b in range(pieces)]
    gains = jnp.concatenate(
        [gain_g.reshape(count, rows), gain_ffn_g.reshape(count, rows)], axis=1
    ).astype(bf16)
    gains = jnp.pad(gains[:, None, :], ((0, 0), (0, 7), (0, width - 2 * rows)))
    return jnp.concatenate(
        [
            value_g.reshape(count, rows, width),
            out_g.reshape(count, rows, width),
            *ups,
            down_g.reshape(count, pieces * rows, width),
            gains,
        ],
        axis=1,
    )


def unpack_grads(packed, rows, pieces):
    packed = packed.astype(f32)
    low = (2 + pieces) * rows
    ups = [packed[(2 + b) * rows : (3 + b) * rows] for b in range(pieces)]
    gains = packed[low + pieces * rows]
    return (
        gains[:rows],
        packed[:rows],
        packed[rows : 2 * rows],
        gains[rows : 2 * rows],
        jnp.concatenate(ups, axis=1),
        packed[low : low + pieces * rows],
    )


def local(
    inputs, lengths, prenorm, value_proj, mixing, out_proj, ffn_gain, up_proj, down_proj, cotangent
):
    layers, rows, width = value_proj.shape
    pieces = up_proj.shape[-1] // width
    count = width // rows
    slots_here = inputs.shape[1]
    heads = mixing.shape[1]
    slots = mixing.shape[3]
    head_dim = width // (heads * (slots // slots_here))
    position = lax.axis_index("pos") * slots_here + lax.iota(jnp.int32, slots_here)
    live = (position < lengths[0]).astype(f32)[:, None]
    all_lengths = lax.all_gather(lengths, "seq", axis=0, tiled=True)
    seqs = all_lengths.shape[0]
    mask = (lax.iota(jnp.int32, slots)[None, :] < all_lengths[:, None]).astype(f32)

    state = inputs[0].astype(f32) * live
    fetched = []
    stored = []
    for which in range(layers):
        packed = pack_weights(
            which, prenorm, value_proj, out_proj, ffn_gain, up_proj, down_proj
        )
        gathered = lax.all_gather(packed, both, axis=0)
        fetched.append(unpack_weights(gathered, rows, pieces))
    for which in range(layers):
        value_w, out_w, up_w, down_w, gain, gain_ffn = fetched[which]
        normed = rms_forward(state, gain)
        valued = dot("de,td->et", value_w, normed).astype(bf16)
        values = lax.all_to_all(valued, "pos", split_axis=0, concat_axis=1, tiled=True)
        values = lax.all_gather(values, "seq", axis=0)
        values = values.reshape(seqs, heads, head_dim, slots)
        raised = jnp.exp(mixing[which].astype(f32)).astype(bf16)
        totals = dot("sj,hij->shi", mask.astype(bf16), raised)
        inverse = 1.0 / totals
        mixed = dot("shdj,hij->shdi", values, raised) * inverse[:, :, None, :]
        mixed = mixed.astype(bf16)
        back = mixed.reshape(seqs, heads * head_dim, mixed.shape[-1])
        back = lax.all_to_all(back, "seq", split_axis=0, concat_axis=2, tiled=True)[0]
        back = lax.all_to_all(back, "pos", split_axis=1, concat_axis=0, tiled=True)
        returned = (back.T.astype(f32) * live).astype(bf16)
        middle = state + dot("td,de->te", returned, out_w)
        normed_ffn = rms_forward(middle, gain_ffn)
        pre_act = dot("td,df->tf", normed_ffn, up_w)
        activated = gelu_parts(pre_act)[0].astype(bf16)
        stored.append(
            (state, normed, values, raised, inverse, mixed, returned, middle, normed_ffn, pre_act)
        )
        state = middle + dot("tf,fd->td", activated, down_w)

    upstream = cotangent[0].astype(f32) * live
    outcomes = [None] * layers
    logit_grads = [None] * layers
    for which in reversed(range(layers)):
        value_w, out_w, up_w, down_w, gain, gain_ffn = fetched[which]
        before, normed, values, raised, inverse, mixed, returned, middle, normed_ffn, pre_act = (
            stored[which]
        )
        grad_ffn = upstream.astype(bf16)
        activated, slope = gelu_parts(pre_act)
        grad_down = dot("tf,td->fd", activated.astype(bf16), grad_ffn).astype(bf16)
        grad_pre = (dot("td,fd->tf", grad_ffn, down_w) * slope).astype(bf16)
        grad_up = dot("td,tf->df", normed_ffn, grad_pre).astype(bf16)
        step, grad_gain_ffn = rms_backward(middle, gain_ffn, dot("tf,df->td", grad_pre, up_w))
        grad_middle = upstream + step
        grad_mid = grad_middle.astype(bf16)
        grad_out = dot("td,te->de", returned, grad_mid).astype(bf16)
        grad_mixed = dot("ed,td->et", out_w, grad_mid).astype(bf16)
        sent = lax.all_to_all(grad_mixed, "pos", split_axis=0, concat_axis=1, tiled=True)
        sent = sent[None]
        grads = lax.all_to_all(sent, "seq", split_axis=2, concat_axis=0, tiled=True)
        grads = grads.reshape(mixed.shape).astype(f32)
        row_sums = jnp.sum(grads * mixed.astype(f32), axis=2) * inverse
        scaled = (grads * inverse[:, :, None, :]).astype(bf16)
        table = dot("shdi,shdj->hij", scaled, values)
        table = table - jnp.einsum(
            "shi,sj->hij", row_sums, mask, precision=lax.Precision.HIGHEST
        )
        logit_grads[which] = raised.astype(f32) * table
        partial = (dot("shdi,hij->shdj", scaled, raised) * mask[:, None, None, :]).astype(bf16)
        partial = partial.reshape(seqs, heads * head_dim, slots)
        summed = lax.psum_scatter(partial, "seq", scatter_dimension=0, tiled=True)[0]
        grad_valued = lax.all_to_all(summed, "pos", split_axis=1, concat_axis=0, tiled=True)
        grad_value = dot("td,et->de", normed, grad_valued).astype(bf16)
        step, grad_gain = rms_backward(before, gain, dot("et,de->td", grad_valued, value_w))
        upstream = grad_middle + step
        packed = pack_grads(
            grad_value, grad_out, grad_up, grad_down, grad_gain, grad_gain_ffn, count
        )
        reduced = lax.psum_scatter(packed, both, scatter_dimension=0, tiled=True)[0]
        outcomes[which] = unpack_grads(reduced, rows, pieces)
    merged = [jnp.stack([terms[member] for terms in outcomes]) for member in range(6)]
    return (
        state.astype(bf16)[None],
        (upstream * live).astype(bf16)[None],
        merged[0],
        merged[1],
        jnp.stack(logit_grads),
        merged[2],
        merged[3],
        merged[4],
        merged[5],
    )


def split_columns(matrix, width):
    return [matrix[:, low : low + width] for low in range(0, matrix.shape[1], width)]


def from_slices(packed, low, rows, width):
    return packed[:, low : low + rows].reshape(-1, width)


def to_slices(matrix, count):
    return matrix.reshape(count, -1, matrix.shape[-1])


def local_direct(
    inputs, lengths, prenorm, value_proj, mixing, out_proj, ffn_gain, up_proj, down_proj, cotangent
):
    layers, rows, width = value_proj.shape
    pieces = up_proj.shape[-1] // width
    count = width // rows
    slots_here = inputs.shape[1]
    heads, rows_here, slots = mixing.shape[1:]
    head_dim = width // (heads * 4)
    seqs = 8
    position = lax.axis_index("pos") * slots_here + lax.iota(jnp.int32, slots_here)
    live = (position < lengths[0]).astype(f32)[:, None]
    swap = []
    for seq in range(8):
        for pos in range(4):
            there = (seq - seq % 2 + pos % 2, pos - pos % 2 + seq % 2)
            swap.append((4 * seq + pos, 4 * there[0] + there[1]))
    logits = lax.ppermute(mixing, both, swap)

    high = lengths // 32
    small = jnp.concatenate(
        [prenorm.reshape(-1), ffn_gain.reshape(-1), high.astype(bf16), (lengths - 32 * high).astype(bf16)]
    )
    small = jnp.pad(small[None, :], ((0, 7), (0, width - small.shape[0])))
    (first,) = gather(jnp.concatenate([value_proj[0], small]), None, 0)
    value_w = [from_slices(first, 0, rows, width), None]
    small = first[:, rows].astype(f32)
    gains = small[:, : 4 * rows].reshape(count, 4, rows).transpose(1, 0, 2).reshape(4, width)
    told = small[:, 4 * rows : 4 * rows + 2]
    told = (told[:, 0] * 32.0 + told[:, 1]).astype(jnp.int32)
    all_lengths = told.reshape(seqs, -1)[:, 0]
    mask = (lax.iota(jnp.int32, slots)[None, :] < all_lengths[:, None]).astype(f32)

    state = inputs[0].astype(f32) * live
    fetched = []
    stored = []
    for which in range(layers):
        gain, gain_ffn = gains[which], gains[layers + which]
        normed = rms_forward(state, gain)
        valued = dot("de,td->et", value_w[which], normed).astype(bf16)
        valued = valued.reshape(4, heads, head_dim, slots_here)
        packed = [out_proj[which], *split_columns(up_proj[which], width), down_proj[which]]
        if which + 1 < layers:
            packed.append(value_proj[which + 1])
        gathered, values = gather(jnp.concatenate(packed), valued, 1 + which)
        out_w = from_slices(gathered, 0, rows, width)
        ups = [from_slices(gathered, (1 + b) * rows, rows, width) for b in range(pieces)]
        up_w = jnp.concatenate(ups, axis=1)
        down_w = from_slices(gathered, (1 + pieces) * rows, pieces * rows, width)
        if which + 1 < layers:
            value_w[which + 1] = from_slices(gathered, (1 + 2 * pieces) * rows, rows, width)
        fetched.append((out_w, up_w, down_w))
        raised = jnp.exp(logits[which].astype(f32)).astype(bf16)
        totals = dot("sj,hij->hsi", mask.astype(bf16), raised)
        inverse = 1.0 / totals
        mixed = dot("hsj,hij->hsi", values, raised).reshape(heads, seqs, head_dim, rows_here)
        mixed = (mixed * inverse[:, :, None, :]).astype(bf16)
        returned = trade(mixed, False, 3 + which).reshape(width, slots_here)
        returned = (returned.astype(f32) * live[:, 0]).astype(bf16)
        middle = state + dot("dt,de->te", returned, out_w)
        normed_ffn = rms_forward(middle, gain_ffn)
        pre_act = dot("td,df->tf", normed_ffn, up_w)
        activated = gelu_parts(pre_act)[0].astype(bf16)
        stored.append(
            (state, normed, values, raised, inverse, mixed, returned, middle, normed_ffn, pre_act)
        )
        state = middle + dot("tf,fd->td", activated, down_w)

    upstream = cotangent[0].astype(f32) * live
    value_g, gain_g, reduced, logit_g = [None] * layers, [None] * layers, [None] * layers, [None] * layers
    for which in reversed(range(layers)):
        gain, gain_ffn = gains[which], gains[layers + which]
        out_w, up_w, down_w = fetched[which]
        before, normed, values, raised, inverse, mixed, returned, middle, normed_ffn, pre_act = (
            stored[which]
        )
        grad_ffn = upstream.astype(bf16)
        activated, slope = gelu_parts(pre_act)
        grad_down = dot("tf,td->fd", activated.astype(bf16), grad_ffn).astype(bf16)
        grad_pre = (dot("td,fd->tf", grad_ffn, down_w) * slope).astype(bf16)
        grad_up = dot("td,tf->df", normed_ffn, grad_pre).astype(bf16)
        step, grad_gain_ffn = rms_backward(middle, gain_ffn, dot("tf,df->td", grad_pre, up_w))
        grad_middle = upstream + step
        grad_mid = grad_middle.astype(bf16)
        grad_out = dot("dt,te->de", returned, grad_mid).astype(bf16)
        grad_mixed = dot("ed,td->et", out_w, grad_mid).astype(bf16)
        grads = trade(grad_mixed.reshape(4, heads, head_dim, slots_here), True, 5 + which)
        grads = grads.astype(f32)
        row_sums = jnp.sum(grads * mixed.astype(f32), axis=2) * inverse
        scaled = (grads * inverse[:, :, None, :]).astype(bf16)
        scaled = scaled.reshape(heads, seqs * head_dim, rows_here)
        partial = dot("hsi,hij->hsj", scaled, raised).reshape(heads, seqs, head_dim, slots)
        partial = (partial * mask[None, :, None, :]).astype(bf16)
        packed = [
            to_slices(grad_out, count),
            *[to_slices(part, count) for part in split_columns(grad_up, width)],
            to_slices(grad_down, count),
        ]
        if which + 1 < layers:
            packed.append(to_slices(value_g[which + 1], count))
        else:
            packed.append(jnp.zeros((count, 8, width), bf16))
        partial = partial.reshape(heads, seqs * head_dim, slots)
        reduced[which], grad_valued = reduce(jnp.concatenate(packed, axis=1), partial, 7 + which)
        table = dot("hsi,hsj->hij", scaled, values)
        table = table - jnp.einsum("hsi,sj->hij", row_sums, mask, precision=lax.Precision.HIGHEST)
        logit_g[which] = lax.ppermute((raised.astype(f32) * table).astype(bf16), both, swap)
        grad_valued = grad_valued.reshape(width, slots_here)
        value_g[which] = dot("td,et->de", normed, grad_valued).astype(bf16)
        step, grad_gain = rms_backward(before, gain, dot("et,de->td", grad_valued, value_w[which]))
        gain_g[which] = (grad_gain, grad_gain_ffn)
        upstream = grad_middle + step

    small = jnp.stack([gain_g[0][0], gain_g[1][0], gain_g[0][1], gain_g[1][1]])
    small = small.reshape(4, count, rows).transpose(1, 0, 2).reshape(count, 1, 4 * rows)
    small = jnp.pad(small.astype(bf16), ((0, 0), (0, 7), (0, width - 4 * rows)))
    (last,) = reduce(jnp.concatenate([to_slices(value_g[0], count), small], axis=1), None, 9)
    small = last[rows, : 4 * rows].reshape(2, layers, rows)
    low = (1 + 2 * pieces) * rows

    def up_part(packed):
        return jnp.concatenate(
            [packed[(1 + b) * rows : (2 + b) * rows] for b in range(pieces)], axis=1
        )

    return (
        state.astype(bf16)[None],
        (upstream * live).astype(bf16)[None],
        small[0],
        jnp.stack([last[:rows], reduced[0][low : low + rows]]),
        jnp.stack(logit_g).astype(f32),
        jnp.stack([packed[:rows] for packed in reduced]),
        small[1],
        jnp.stack([up_part(packed) for packed in reduced]),
        jnp.stack([packed[(1 + pieces) * rows : low] for packed in reduced]),
    )


def solution(mesh):
    direct = mesh.shape["seq"] == 8 and mesh.shape["pos"] == 4
    return jax.shard_map(
        local_direct if direct else local,
        mesh=mesh,
        in_specs=(
            P("seq", "pos", None),
            P("seq"),
            P(None, ("seq", "pos")),
            P(None, ("seq", "pos"), None),
            P(None, "pos", "seq", None),
            P(None, ("seq", "pos"), None),
            P(None, ("seq", "pos")),
            P(None, ("seq", "pos"), None),
            P(None, ("seq", "pos"), None),
            P("seq", "pos", None),
        ),
        out_specs=(
            P("seq", "pos", None),
            P("seq", "pos", None),
            P(None, ("seq", "pos")),
            P(None, ("seq", "pos"), None),
            P(None, "pos", "seq", None),
            P(None, ("seq", "pos"), None),
            P(None, ("seq", "pos")),
            P(None, ("seq", "pos"), None),
            P(None, ("seq", "pos"), None),
        ),
        check_vma=False,
    )
```
